512 devices in a mesh: img: 32 (over z, y_hi), comp: 2 (over y_lo), ref: 8 (over x, core).
Axes of the slice: x: 4, y: 4 (y_hi: 2, y_lo: 2; y = y_hi * 2 + y_lo), z: 16, core: 2. Of those that a mesh axis runs over, the one named last changes fastest.
Arguments:
- images: float32 [3072, 16384], P('img', 'comp'), may hold values from -24 to 24
- references: float32 [2048, 16384], P(('img', 'ref'), 'comp'), may hold values from -0.140625 to 0.140625
Outputs:
- weighted_sums: float32 [2048, 16384], P(('img', 'ref'), 'comp')
The draws below stay inside these ranges and needn't reach their ends.
All inputs are finite; a program needn't handle non-finite values.
Results may differ from the reference program's by a relative error of at most 0.0003.
Values sent between devices are 32-bit elements; how exact they have to be, the bound alone decides.
No kernel may reach another device: no remote copies, remote signals or barrier semaphores. Data moves between devices by JAX's collectives and lax.ppermute only.
A program may use at most 64 MiB of HBM per device.

```python
import math
import jax
import jax.numpy as jnp
from jax import lax

K = 16384
NIMG = 3072
NREF = 2048


def base_refs(key):
    return jnp.clip(jax.random.normal(jax.random.fold_in(key, 11), (NREF, K), jnp.float32), -6.0, 6.0)


def draw_references(key, part):
    return base_refs(key) * (3.0 / math.sqrt(K))


def draw_images(key, part):
    noise_key = jax.random.fold_in(key, 23)
    noise = jnp.clip(jax.random.normal(noise_key, (NIMG, K), jnp.float32), -6.0, 6.0)
    base = base_refs(key)
    first = jax.random.randint(jax.random.fold_in(key, 31), (NIMG,), 0, NREF)
    second = (first + jax.random.randint(jax.random.fold_in(key, 37), (NIMG,), 1, NREF)) % NREF
    levels = jnp.array([120.0, 200.0, 300.0], jnp.float32)
    level = levels[jax.random.randint(jax.random.fold_in(key, 41), (NIMG,), 0, 3)]
    factor = level / (3.0 * math.sqrt(K))
    chosen = jax.random.bernoulli(jax.random.fold_in(key, 43), 0.1, (NIMG,))
    aligned = jnp.clip(factor[:, None] * (base[first] + base[second]), -24.0, 24.0)
    return jnp.where(chosen[:, None], aligned, noise)


def setup_inputs(seed: int = 0) -> dict:
    key_list = jax.random.split(jax.random.key(seed), 3)
    images = draw_images(jax.random.fold_in(key_list[2], 71), 0)
    references = draw_references(jax.random.fold_in(key_list[2], 71), 0)
    return dict(images=images, references=references)


def reference(images, references):
    highest = lax.Precision.HIGHEST
    scores = jnp.dot(images, references.T, precision=highest, preferred_element_type=jnp.float32)
    scores = scores - 0.5 * jnp.sum(references * references, axis=1)[None, :]
    largest = jnp.max(scores, axis=1)
    expon = jnp.exp(scores - largest[:, None])
    totals = jnp.sum(expon, axis=1)
    posterior = expon / totals[:, None]
    return jnp.dot(posterior.T, images, precision=highest, preferred_element_type=jnp.float32)
```

```python
import jax
import jax.numpy as jnp
from jax import lax
from jax.sharding import Mesh, PartitionSpec as P

HIGHEST = lax.Precision.HIGHEST
PLANE = ("core", "yl", "x")
OWNERS = ("yh", "x", "core")
CHUNKS = (64, 32)


def shards(images, references):
    count_z = lax.axis_size("z")
    slices = lax.axis_size("x") * lax.axis_size("core")
    width = images.shape[1] // slices
    mine = lax.axis_index(("x", "core"))
    own = lax.dynamic_slice_in_dim(images, mine * width, width, 1)

    pieces = references.reshape(references.shape[0], slices, width).transpose(1, 0, 2)
    half = lax.all_to_all(pieces, ("x", "core"), 0, 0, tiled=True)
    plane_refs = lax.all_gather(half, "yh").reshape(-1, width)
    halfnorm = 0.5 * jnp.sum(plane_refs * plane_refs, axis=1)

    def scores_of(gathered):
        partial = lax.dot_general(
            gathered.reshape(-1, width), plane_refs, (((1,), (1,)), ((), ())),
            precision=HIGHEST, preferred_element_type=jnp.float32)
        partial = (partial - halfnorm[None, :]).reshape(count_z, -1, plane_refs.shape[0])
        return jnp.sum(lax.all_to_all(partial, PLANE, 0, 0, tiled=False), axis=0)

    def posterior_of(scores):
        largest = jnp.max(scores, axis=1)
        expon = jnp.exp(scores - largest[:, None])
        totals = jnp.sum(expon, axis=1)
        stats = jnp.stack([largest, totals])
        everyone = lax.all_to_all(
            jnp.broadcast_to(stats[None], (count_z,) + stats.shape), "z", 0, 0, tiled=False)
        top = jnp.max(everyone[:, 0], axis=0)
        total = jnp.sum(everyone[:, 1] * jnp.exp(everyone[:, 0] - top), axis=0)
        post = expon * (jnp.exp(largest - top) / total)[:, None]
        chips = lax.axis_size("yl") * lax.axis_size("x")
        spread = lax.all_to_all(
            jnp.broadcast_to(post[None], (chips,) + post.shape), ("yl", "x"), 0, 0, tiled=False)
        return lax.all_gather(spread, "core").reshape(-1, post.shape[1])

    out = None
    start = 0
    for rows in CHUNKS:
        part = lax.slice_in_dim(own, start, start + rows, axis=0)
        start += rows
        gathered = lax.all_gather(part, "z")
        post = posterior_of(scores_of(gathered))
        term = lax.dot_general(
            post, gathered.reshape(-1, width), (((0,), (0,)), ((), ())),
            precision=HIGHEST, preferred_element_type=jnp.float32)
        out = term if out is None else out + term

    owners = lax.axis_size("yh") * slices
    back = lax.all_to_all(out.reshape(owners, -1, width), OWNERS, 0, 0, tiled=False)
    rows = jnp.sum(back.reshape(lax.axis_size("yh"), slices, -1, width), axis=0)
    return rows.transpose(1, 0, 2).reshape(references.shape)


def solution(mesh):
    fine = Mesh(mesh.devices.reshape(16, 2, 2, 4, 2), ("z", "yh", "yl", "x", "core"))
    return jax.shard_map(
        shards,
        mesh=fine,
        in_specs=(P(("z", "yh"), "yl"), P(("z", "yh", "x", "core"), "yl")),
        out_specs=P(("z", "yh", "x", "core"), "yl"),
        check_vma=False,
    )
```

```python
import jax
import jax.numpy as jnp
from jax import lax
from jax.sharding import Mesh, PartitionSpec as P

HIGHEST = lax.Precision.HIGHEST
PLANE = ("core", "yl", "x")
OWNERS = ("yh", "x", "core")


def turned(value, steps):
    count = lax.axis_size("z")
    return lax.ppermute(value, "z", [(i, (i + steps) % count) for i in range(count)])


def shards(images, references):
    count_z = lax.axis_size("z")
    slices = lax.axis_size("x") * lax.axis_size("core")
    width = images.shape[1] // slices
    mine = lax.axis_index(("x", "core"))
    here = lax.axis_index("z")
    own = lax.dynamic_slice_in_dim(images, mine * width, width, 1)
    rows = own.shape[0]

    pieces = references.reshape(references.shape[0], slices, width).transpose(1, 0, 2)
    half = lax.all_to_all(pieces, ("x", "core"), 0, 0, tiled=True)
    plane_refs = lax.all_gather(half, "yh").reshape(-1, width)
    halfnorm = 0.5 * jnp.sum(plane_refs * plane_refs, axis=1)

    gathered = jnp.zeros((count_z * rows, width), jnp.float32)
    partial = jnp.zeros((count_z * rows, plane_refs.shape[0]), jnp.float32)

    def place(gathered, partial, block, offset, first_row):
        scores = lax.dot_general(
            block, plane_refs, (((1,), (1,)), ((), ())),
            precision=HIGHEST, preferred_element_type=jnp.float32) - halfnorm[None, :]
        at = (here + offset) % count_z * rows + first_row
        return (lax.dynamic_update_slice_in_dim(gathered, block, at, 0),
                lax.dynamic_update_slice_in_dim(partial, scores, at, 0))

    gathered, partial = place(gathered, partial, own, 0, 0)
    right = left = own
    for step in range(1, count_z // 2 + 1):
        if step < count_z // 2:
            right, left = turned(right, 1), turned(left, -1)
            gathered, partial = place(gathered, partial, right, -step, 0)
            gathered, partial = place(gathered, partial, left, step, 0)
        else:
            cut = rows // 2
            right, left = turned(right[:cut], 1), turned(left[cut:], -1)
            gathered, partial = place(gathered, partial, right, -step, 0)
            gathered, partial = place(gathered, partial, left, step, cut)

    partial = partial.reshape(count_z, rows, -1)
    scores = jnp.sum(lax.all_to_all(partial, PLANE, 0, 0, tiled=False), axis=0)

    largest = jnp.max(scores, axis=1)
    expon = jnp.exp(scores - largest[:, None])
    totals = jnp.sum(expon, axis=1)
    stats = jnp.stack([largest, totals])
    everyone = lax.all_to_all(
        jnp.broadcast_to(stats[None], (count_z,) + stats.shape), "z", 0, 0, tiled=False)
    top = jnp.max(everyone[:, 0], axis=0)
    total = jnp.sum(everyone[:, 1] * jnp.exp(everyone[:, 0] - top), axis=0)
    post = expon * (jnp.exp(largest - top) / total)[:, None]
    chips = lax.axis_size("yl") * lax.axis_size("x")
    spread = lax.all_to_all(
        jnp.broadcast_to(post[None], (chips,) + post.shape), ("yl", "x"), 0, 0, tiled=False)
    post = lax.all_gather(spread, "core").reshape(-1, post.shape[1])

    out = lax.dot_general(
        post, gathered, (((0,), (0,)), ((), ())),
        precision=HIGHEST, preferred_element_type=jnp.float32)

    owners = lax.axis_size("yh") * slices
    back = lax.all_to_all(out.reshape(owners, -1, width), OWNERS, 0, 0, tiled=False)
    mine_rows = jnp.sum(back.reshape(lax.axis_size("yh"), slices, -1, width), axis=0)
    return mine_rows.transpose(1, 0, 2).reshape(references.shape)


def solution(mesh):
    fine = Mesh(mesh.devices.reshape(16, 2, 2, 4, 2), ("z", "yh", "yl", "x", "core"))
    return jax.shard_map(
        shards,
        mesh=fine,
        in_specs=(P(("z", "yh"), "yl"), P(("z", "yh", "x", "core"), "yl")),
        out_specs=P(("z", "yh", "x", "core"), "yl"),
        check_vma=False,
    )
```

```python
import jax
import jax.numpy as jnp
from jax import lax
from jax.sharding import Mesh, PartitionSpec as P

HIGHEST = lax.Precision.HIGHEST
PLANE = ("core", "yl", "x")
OWNERS = ("b", "yh", "x", "core")


def turned(value, axis, steps):
    count = lax.axis_size(axis)
    return lax.ppermute(value, axis, [(i, (i + steps) % count) for i in range(count)])


def both(value, axis):
    other = turned(value, axis, 1)
    first = lax.axis_index(axis) == 0
    return jnp.stack([jnp.where(first, value, other), jnp.where(first, other, value)])


def shards(images, references):
    count = lax.axis_size("q")
    slices = lax.axis_size("x") * lax.axis_size("core")
    width = images.shape[1] // slices
    mine = lax.axis_index(("x", "core"))
    here = lax.axis_index("q")
    own = lax.dynamic_slice_in_dim(images, mine * width, width, 1)
    rows = own.shape[0]
    own, references = lax.optimization_barrier((own, references))

    ref_rows = references.shape[0]
    pair = both(references, "b")
    pieces = pair.reshape(2, ref_rows, slices, width).transpose(2, 0, 1, 3)
    half = lax.all_to_all(pieces, ("x", "core"), 0, 0, tiled=True)
    group_refs = both(half, "yh")
    group_refs = group_refs.transpose(2, 0, 1, 3, 4).reshape(-1, width)
    halfnorm = 0.5 * jnp.sum(group_refs * group_refs, axis=1)

    gathered = jnp.zeros((count * rows, width), jnp.float32)
    partial = jnp.zeros((count * rows, group_refs.shape[0]), jnp.float32)

    def place(gathered, partial, block, offset, first_row):
        scores = lax.dot_general(
            block, group_refs, (((1,), (1,)), ((), ())),
            precision=HIGHEST, preferred_element_type=jnp.float32) - halfnorm[None, :]
        at = (here + offset) % count * rows + first_row
        return (lax.dynamic_update_slice_in_dim(gathered, block, at, 0),
                lax.dynamic_update_slice_in_dim(partial, scores, at, 0))

    gathered, partial = place(gathered, partial, own, 0, 0)
    right = left = own
    for step in range(1, count // 2 + 1):
        if step < count // 2:
            right, left = turned(right, "q", 1), turned(left, "q", -1)
            gathered, partial = place(gathered, partial, right, -step, 0)
            gathered, partial = place(gathered, partial, left, step, 0)
        else:
            cut = rows // 2
            right, left = turned(right[:cut], "q", 1), turned(left[cut:], "q", -1)
            gathered, partial = place(gathered, partial, right, -step, 0)
            gathered, partial = place(gathered, partial, left, step, cut)

    plane = lax.axis_size("yl") * slices
    partial = partial.reshape(plane, -1, group_refs.shape[0])
    scores = jnp.sum(lax.all_to_all(partial, PLANE, 0, 0, tiled=False), axis=0)

    largest = jnp.max(scores, axis=1)
    expon = jnp.exp(scores - largest[:, None])
    totals = jnp.sum(expon, axis=1)
    stats = jnp.stack([largest, totals])
    everyone = lax.all_to_all(
        jnp.broadcast_to(stats[None], (count,) + stats.shape), "q", 0, 0, tiled=False)
    top = jnp.max(everyone[:, 0], axis=0)
    total = jnp.sum(everyone[:, 1] * jnp.exp(everyone[:, 0] - top), axis=0)
    post = expon * (jnp.exp(largest - top) / total)[:, None]
    chips = lax.axis_size("yl") * lax.axis_size("x")
    spread = lax.all_to_all(
        jnp.broadcast_to(post[None], (chips,) + post.shape), ("yl", "x"), 0, 0, tiled=False)
    post = lax.all_gather(spread, "core").reshape(-1, post.shape[1])

    out = lax.dot_general(
        post, gathered, (((0,), (0,)), ((), ())),
        precision=HIGHEST, preferred_element_type=jnp.float32)

    back = lax.all_to_all(
        out.reshape(4 * slices, ref_rows, width), OWNERS, 0, 0, tiled=False)
    mine_rows = jnp.sum(back.reshape(4, slices, ref_rows, width), axis=0)
    return mine_rows.transpose(1, 0, 2).reshape(references.shape)


def solution(mesh):
    fine = Mesh(mesh.devices.reshape(8, 2, 2, 2, 4, 2), ("q", "b", "yh", "yl", "x", "core"))
    return jax.shard_map(
        shards,
        mesh=fine,
        in_specs=(P(("q", "b", "yh"), "yl"), P(("q", "b", "yh", "x", "core"), "yl")),
        out_specs=P(("q", "b", "yh", "x", "core"), "yl"),
        check_vma=False,
    )
```

```python
import jax
import jax.numpy as jnp
from jax import lax
from jax.experimental import pallas as pl
from jax.experimental.pallas import tpu as pltpu
from jax.sharding import Mesh, PartitionSpec as P


HIGHEST = lax.Precision.HIGHEST
PLANE = ("core", "yl", "x")
OWNERS = ("b", "yh", "x", "core")


def turned(value, axis, steps):
    count = lax.axis_size(axis)
    return lax.ppermute(value, axis, [(i, (i + steps) % count) for i in range(count)])


def both(value, axis):
    other = turned(value, axis, 1)
    first = lax.axis_index(axis) == 0
    return jnp.stack([jnp.where(first, value, other), jnp.where(first, other, value)])


def weighted_kernel(at_ref, post_ref, *refs):
    count = at_ref.shape[0]
    blocks, (out_ref, held, sems) = refs[:count], refs[count:]
    copies = []
    for k, block in enumerate(blocks):
        row = pl.multiple_of(at_ref[k], 8)
        copies.append(pltpu.make_async_copy(
            block, held.at[pl.ds(row, block.shape[0])], sems.at[k]))
        copies[-1].start()
    for copy in copies:
        copy.wait()
    post = post_ref[...].T
    tile = 256

    @pl.loop(0, out_ref.shape[1] // tile)
    def _(t):
        columns = pl.ds(pl.multiple_of(t * tile, tile), tile)
        out_ref[:, columns] = jnp.dot(
            post, held[:, columns], precision=HIGHEST,
            preferred_element_type=jnp.float32)


def weighted(at, post, blocks):
    images, refs = post.shape
    width = blocks[0].shape[1]
    return pl.pallas_call(
        weighted_kernel,
        out_shape=jax.ShapeDtypeStruct((refs, width), jnp.float32),
        in_specs=[pl.BlockSpec(memory_space=pltpu.SMEM),
                  pl.BlockSpec(memory_space=pltpu.VMEM)]
        + [pl.BlockSpec(memory_space=pl.ANY)] * len(blocks),
        out_specs=pl.BlockSpec(memory_space=pltpu.VMEM),
        scratch_shapes=[pltpu.VMEM((images, width), jnp.float32),
                        pltpu.SemaphoreType.DMA((len(blocks),))],
        compiler_params=pltpu.CompilerParams(vmem_limit_bytes=24 << 20),
        cost_estimate=pl.CostEstimate(
            flops=12 * images * refs * width, bytes_accessed=8 * images * width,
            transcendentals=0),
        name="weighted",
    )(at, post, *blocks)


def step_on_shards(images, references):
    count = lax.axis_size("q")
    slices = lax.axis_size("x") * lax.axis_size("core")
    width = images.shape[1] // slices
    mine = lax.axis_index(("x", "core"))
    here = lax.axis_index("q")
    own = lax.dynamic_slice_in_dim(images, mine * width, width, 1)
    rows = own.shape[0]

    ref_rows = references.shape[0]
    pair = both(references, "b")
    pieces = pair.reshape(2, ref_rows, slices, width).transpose(2, 0, 1, 3)
    half = lax.all_to_all(pieces, ("x", "core"), 0, 0, tiled=True)
    group_refs = both(half, "yh")
    group_refs = group_refs.transpose(2, 0, 1, 3, 4).reshape(-1, width)
    halfnorm = 0.5 * jnp.sum(group_refs * group_refs, axis=1)

    partial = jnp.zeros((count * rows, group_refs.shape[0]), jnp.float32)
    blocks, offsets, firsts = [], [], []

    def place(partial, block, offset, first_row):
        scores = lax.dot_general(
            block, group_refs, (((1,), (1,)), ((), ())),
            precision=HIGHEST, preferred_element_type=jnp.float32) - halfnorm[None, :]
        row = (here + offset) % count * rows + first_row
        blocks.append(block)
        offsets.append(offset)
        firsts.append(first_row)
        return lax.dynamic_update_slice_in_dim(partial, scores, row, 0)

    partial = place(partial, own, 0, 0)
    right = left = own
    last = count // 2
    for step in range(1, last):
        right = turned(right, "q", 1)
        left = turned(left, "q", -1)
        if step == last - 1:
            partial, right_end, left_end = lax.optimization_barrier((partial, right, left))
            cut = rows // 2
            right_end = turned(right_end[:cut], "q", 1)
            left_end = turned(left_end[cut:], "q", -1)
        partial = place(partial, right, -step, 0)
        partial = place(partial, left, step, 0)
    partial = place(partial, right_end, -last, 0)
    partial = place(partial, left_end, last, cut)

    plane = lax.axis_size("yl") * slices
    partial = partial.reshape(plane, -1, group_refs.shape[0])
    scores = jnp.sum(lax.all_to_all(partial, PLANE, 0, 0, tiled=False), axis=0)

    largest = jnp.max(scores, axis=1)
    expon = jnp.exp(scores - largest[:, None])
    totals = jnp.sum(expon, axis=1)
    stats = jnp.stack([largest, totals])
    everyone = lax.all_to_all(
        jnp.broadcast_to(stats[None], (count,) + stats.shape), "q", 0, 0, tiled=False)
    top = jnp.max(everyone[:, 0], axis=0)
    total = jnp.sum(everyone[:, 1] * jnp.exp(everyone[:, 0] - top), axis=0)
    post = expon * (jnp.exp(largest - top) / total)[:, None]
    chips = lax.axis_size("yl") * lax.axis_size("x")
    spread = lax.all_to_all(
        jnp.broadcast_to(post[None], (chips,) + post.shape), ("yl", "x"), 0, 0, tiled=False)
    post = lax.all_gather(spread, "core").reshape(-1, post.shape[1])

    at = (here + jnp.array(offsets, jnp.int32)) % count * rows + jnp.array(firsts, jnp.int32)
    out = weighted(at, post, blocks)

    back = lax.all_to_all(
        out.reshape(4 * slices, ref_rows, width), OWNERS, 0, 0, tiled=False)
    mine_rows = jnp.sum(back.reshape(4, slices, ref_rows, width), axis=0)
    return mine_rows.transpose(1, 0, 2).reshape(references.shape)


def solution(mesh):
    fine = Mesh(mesh.devices.reshape(8, 2, 2, 2, 4, 2), ("q", "b", "yh", "yl", "x", "core"))
    return jax.shard_map(
        step_on_shards,
        mesh=fine,
        in_specs=(P(("q", "b", "yh"), "yl"), P(("q", "b", "yh", "x", "core"), "yl")),
        out_specs=P(("q", "b", "yh", "x", "core"), "yl"),
        check_vma=False,
    )
```

```python
import jax
import jax.numpy as jnp
from jax import lax
from jax.sharding import Mesh, PartitionSpec as P

HIGHEST = lax.Precision.HIGHEST
PLANE = ("core", "yl", "x")
OWNERS = ("yh", "x", "core")


def moved(value, axis, steps):
    count = lax.axis_size(axis)
    return lax.ppermute(value, axis, [(i, (i + steps) % count) for i in range(count)])


def turned(value, steps):
    return moved(value, "z", steps)


def both(value, axis):
    other = moved(value, axis, 1)
    first = lax.axis_index(axis) == 0
    return jnp.stack([jnp.where(first, value, other), jnp.where(first, other, value)])


def shards(images, references):
    count_z = lax.axis_size("z")
    slices = lax.axis_size("x") * lax.axis_size("core")
    width = images.shape[1] // slices
    mine = lax.axis_index(("x", "core"))
    here = lax.axis_index("z")
    own = lax.optimization_barrier(lax.dynamic_slice_in_dim(images, mine * width, width, 1))
    rows = own.shape[0]

    pieces = references.reshape(references.shape[0], slices, width).transpose(1, 0, 2)
    half = lax.all_to_all(pieces, ("x", "core"), 0, 0, tiled=True)
    plane_refs = both(half, "yh").reshape(-1, width)
    halfnorm = 0.5 * jnp.sum(plane_refs * plane_refs, axis=1)

    gathered = jnp.zeros((count_z * rows, width), jnp.float32)
    partial = jnp.zeros((count_z * rows, plane_refs.shape[0]), jnp.float32)

    def place(gathered, partial, block, offset, first_row):
        scores = lax.dot_general(
            block, plane_refs, (((1,), (1,)), ((), ())),
            precision=HIGHEST, preferred_element_type=jnp.float32) - halfnorm[None, :]
        at = (here + offset) % count_z * rows + first_row
        return (lax.dynamic_update_slice_in_dim(gathered, block, at, 0),
                lax.dynamic_update_slice_in_dim(partial, scores, at, 0))

    gathered, partial = place(gathered, partial, own, 0, 0)
    right = left = own
    for step in range(1, count_z // 2 + 1):
        if step < count_z // 2:
            right, left = turned(right, 1), turned(left, -1)
            gathered, partial = place(gathered, partial, right, -step, 0)
            gathered, partial = place(gathered, partial, left, step, 0)
        else:
            cut = rows // 2
            right, left = turned(right[:cut], 1), turned(left[cut:], -1)
            gathered, partial = place(gathered, partial, right, -step, 0)
            gathered, partial = place(gathered, partial, left, step, cut)

    partial = partial.reshape(count_z, rows, -1)
    scores = jnp.sum(lax.all_to_all(partial, PLANE, 0, 0, tiled=False), axis=0)

    largest = jnp.max(scores, axis=1)
    expon = jnp.exp(scores - largest[:, None])
    totals = jnp.sum(expon, axis=1)
    stats = jnp.stack([largest, totals])
    everyone = lax.all_to_all(
        jnp.broadcast_to(stats[None], (count_z,) + stats.shape), "z", 0, 0, tiled=False)
    top = jnp.max(everyone[:, 0], axis=0)
    total = jnp.sum(everyone[:, 1] * jnp.exp(everyone[:, 0] - top), axis=0)
    post = expon * (jnp.exp(largest - top) / total)[:, None]
    chips = lax.axis_size("yl") * lax.axis_size("x")
    spread = lax.all_to_all(
        jnp.broadcast_to(post[None], (chips,) + post.shape), ("yl", "x"), 0, 0, tiled=False)
    post = lax.all_gather(spread, "core").reshape(-1, post.shape[1])

    out = lax.dot_general(
        post, gathered, (((0,), (0,)), ((), ())),
        precision=lax.Precision.HIGH, preferred_element_type=jnp.float32)

    owners = lax.axis_size("yh") * slices
    back = lax.all_to_all(out.reshape(owners, -1, width), OWNERS, 0, 0, tiled=False)
    mine_rows = jnp.sum(back.reshape(lax.axis_size("yh"), slices, -1, width), axis=0)
    return mine_rows.transpose(1, 0, 2).reshape(references.shape)


def solution(mesh):
    fine = Mesh(mesh.devices.reshape(16, 2, 2, 4, 2), ("z", "yh", "yl", "x", "core"))
    return jax.shard_map(
        shards,
        mesh=fine,
        in_specs=(P(("z", "yh"), "yl"), P(("z", "yh", "x", "core"), "yl")),
        out_specs=P(("z", "yh", "x", "core"), "yl"),
        check_vma=False,
    )
```

```python
import functools

import jax
import jax.numpy as jnp
from jax import lax
from jax.experimental import pallas as pl
from jax.experimental.pallas import tpu as pltpu
from jax.sharding import Mesh, PartitionSpec as P


HIGHEST = lax.Precision.HIGHEST
PLANE = ("core", "yl", "x")
OWNERS = ("yh", "x", "core")


def moved(value, axis, steps):
    count = lax.axis_size(axis)
    return lax.ppermute(value, axis, [(i, (i + steps) % count) for i in range(count)])


def both(value, axis):
    other = moved(value, axis, 1)
    first = lax.axis_index(axis) == 0
    return jnp.stack([jnp.where(first, value, other), jnp.where(first, other, value)])


def cut_kernel(at_ref, images_ref, out_ref, sem):
    width = out_ref.shape[1]
    columns = pl.ds(pl.multiple_of(at_ref[0] * width, width), width)
    copy = pltpu.make_async_copy(images_ref.at[:, columns], out_ref, sem)
    copy.start()
    copy.wait()


def cut(images, which, width):
    return pl.pallas_call(
        cut_kernel,
        out_shape=jax.ShapeDtypeStruct((images.shape[0], width), jnp.float32),
        in_specs=[pl.BlockSpec(memory_space=pltpu.SMEM),
                  pl.BlockSpec(memory_space=pltpu.HBM)],
        out_specs=pl.BlockSpec(memory_space=pltpu.VMEM),
        scratch_shapes=[pltpu.SemaphoreType.DMA(())],
        name="cut",
    )(which.reshape(1).astype(jnp.int32), images)


def weighted_kernel(starts, at_ref, post_ref, *refs):
    count = len(starts)
    blocks, (out_ref, held, order, sems) = refs[:count], refs[count:]
    copies = []
    for k, block in enumerate(blocks):
        copies.append(pltpu.make_async_copy(
            block, held.at[pl.ds(starts[k], block.shape[0])], sems.at[k]))
        copies[-1].start()
    for k, block in enumerate(blocks):
        size = block.shape[0]
        row = pl.multiple_of(at_ref[k], 8)
        order[starts[k]:starts[k] + size, :] = post_ref[pl.ds(row, size), :]
    tile = 256
    pieces = 3
    part = held.shape[0] // pieces
    waited = 0
    for piece in range(pieces):
        stop = (piece + 1) * part
        while waited < count and starts[waited] < stop:
            copies[waited].wait()
            waited += 1
        rows = pl.ds(piece * part, part)
        post = order[rows, :].T

        @pl.loop(0, out_ref.shape[1] // tile)
        def _(t):
            columns = pl.ds(pl.multiple_of(t * tile, tile), tile)
            term = jnp.dot(post, held[rows, columns], precision=HIGHEST,
                           preferred_element_type=jnp.float32)
            if piece == 0:
                out_ref[:, columns] = term
            else:
                out_ref[:, columns] += term


def weighted(at, post, blocks):
    images, refs = post.shape
    width = blocks[0].shape[1]
    starts = [0]
    for block in blocks[:-1]:
        starts.append(starts[-1] + block.shape[0])
    return pl.pallas_call(
        functools.partial(weighted_kernel, starts),
        out_shape=jax.ShapeDtypeStruct((refs, width), jnp.float32),
        in_specs=[pl.BlockSpec(memory_space=pltpu.SMEM),
                  pl.BlockSpec(memory_space=pltpu.VMEM)]
        + [pl.BlockSpec(memory_space=pl.ANY)] * len(blocks),
        out_specs=pl.BlockSpec(memory_space=pltpu.VMEM),
        scratch_shapes=[pltpu.VMEM((images, width), jnp.float32),
                        pltpu.VMEM((images, refs), jnp.float32),
                        pltpu.SemaphoreType.DMA((len(blocks),))],
        cost_estimate=pl.CostEstimate(
            flops=12 * images * refs * width, bytes_accessed=8 * images * width,
            transcendentals=0),
        name="weighted",
    )(at, post, *blocks)


def step_on_shards(images, references):
    count_z = lax.axis_size("z")
    slices = lax.axis_size("x") * lax.axis_size("core")
    width = images.shape[1] // slices
    here = lax.axis_index("z")
    own = cut(images, lax.axis_index(("x", "core")), width)
    rows = own.shape[0]

    pieces = references.reshape(references.shape[0], slices, width).transpose(1, 0, 2)
    half = lax.all_to_all(pieces, ("x", "core"), 0, 0, tiled=True)
    plane_refs = both(half, "yh").reshape(-1, width)
    halfnorm = 0.5 * jnp.sum(plane_refs * plane_refs, axis=1)

    partial = jnp.zeros((count_z * rows, plane_refs.shape[0]), jnp.float32)
    blocks, offsets, firsts = [], [], []

    def place(partial, block, offset, first_row):
        scores = lax.dot_general(
            block, plane_refs, (((1,), (1,)), ((), ())),
            precision=HIGHEST, preferred_element_type=jnp.float32) - halfnorm[None, :]
        blocks.append(block)
        offsets.append(offset)
        firsts.append(first_row)
        row = (here + offset) % count_z * rows + first_row
        return lax.dynamic_update_slice_in_dim(partial, scores, row, 0)

    partial = place(partial, own, 0, 0)
    right = left = own
    for step in range(1, count_z // 2 + 1):
        middle = 0
        if step == count_z // 2:
            middle = rows // 2
            right, left = right[:middle], left[middle:]
        right = moved(right, "z", 1)
        left = moved(left, "z", -1)
        partial = place(partial, right, -step, 0)
        partial = place(partial, left, step, middle)

    partial = partial.reshape(count_z, rows, -1)
    scores = jnp.sum(lax.all_to_all(partial, PLANE, 0, 0, tiled=False), axis=0)

    largest = jnp.max(scores, axis=1)
    expon = jnp.exp(scores - largest[:, None])
    totals = jnp.sum(expon, axis=1)
    stats = jnp.stack([largest, totals])
    everyone = lax.all_to_all(
        jnp.broadcast_to(stats[None], (count_z,) + stats.shape), "z", 0, 0, tiled=False)
    top = jnp.max(everyone[:, 0], axis=0)
    total = jnp.sum(everyone[:, 1] * jnp.exp(everyone[:, 0] - top), axis=0)
    post = expon * (jnp.exp(largest - top) / total)[:, None]
    chips = lax.axis_size("yl") * lax.axis_size("x")
    spread = lax.all_to_all(
        jnp.broadcast_to(post[None], (chips,) + post.shape), ("yl", "x"), 0, 0, tiled=False)
    post = lax.all_gather(spread, "core").reshape(-1, post.shape[1])

    at = (here + jnp.array(offsets, jnp.int32)) % count_z * rows + jnp.array(firsts, jnp.int32)
    out = weighted(at, post, blocks)

    owners = lax.axis_size("yh") * slices
    back = lax.all_to_all(out.reshape(owners, -1, width), OWNERS, 0, 0, tiled=False)
    mine_rows = jnp.sum(back.reshape(lax.axis_size("yh"), slices, -1, width), axis=0)
    return mine_rows.transpose(1, 0, 2).reshape(references.shape)


def solution(mesh):
    fine = Mesh(mesh.devices.reshape(16, 2, 2, 4, 2), ("z", "yh", "yl", "x", "core"))
    return jax.shard_map(
        step_on_shards,
        mesh=fine,
        in_specs=(P(("z", "yh"), "yl"), P(("z", "yh", "x", "core"), "yl")),
        out_specs=P(("z", "yh", "x", "core"), "yl"),
        check_vma=False,
    )
```

```python
import functools

import jax
import jax.numpy as jnp
from jax import lax
from jax.experimental import pallas as pl
from jax.experimental.pallas import tpu as pltpu
from jax.sharding import Mesh, PartitionSpec as P


HIGHEST = lax.Precision.HIGHEST
PLANE = ("core", "yl", "x")
OWNERS = ("yh", "x", "core")


def moved(value, axis, steps):
    count = lax.axis_size(axis)
    return lax.ppermute(value, axis, [(i, (i + steps) % count) for i in range(count)])


def cut_kernel(at_ref, images_ref, out_ref, sem):
    width = out_ref.shape[1]
    columns = pl.ds(pl.multiple_of(at_ref[0] * width, width), width)
    copy = pltpu.make_async_copy(images_ref.at[:, columns], out_ref, sem)
    copy.start()
    copy.wait()


def cut(images, which, width):
    return pl.pallas_call(
        cut_kernel,
        out_shape=jax.ShapeDtypeStruct((images.shape[0], width), jnp.float32),
        in_specs=[pl.BlockSpec(memory_space=pltpu.SMEM),
                  pl.BlockSpec(memory_space=pltpu.HBM)],
        out_specs=pl.BlockSpec(memory_space=pltpu.VMEM),
        scratch_shapes=[pltpu.SemaphoreType.DMA(())],
        name="cut",
    )(which.reshape(1).astype(jnp.int32), images)


def halves(value):
    high = value.astype(jnp.bfloat16)
    return high, (value - high.astype(jnp.float32)).astype(jnp.bfloat16)


def weighted_kernel(starts, at_ref, post_ref, *refs):
    count = len(starts)
    blocks, (out_ref, held, order, both, sems) = refs[:count], refs[count:]
    tiles = sems.shape[0]
    tile = out_ref.shape[1] // tiles
    copies = []
    for t in range(tiles):
        columns = pl.ds(t * tile, tile)
        copies.append([pltpu.make_async_copy(
            block.at[:, columns], held.at[pl.ds(starts[k], block.shape[0]), columns],
            sems.at[t, k]) for k, block in enumerate(blocks)])
        for copy in copies[-1]:
            copy.start()
    for k, block in enumerate(blocks):
        size = block.shape[0]
        row = pl.multiple_of(at_ref[k], 8)
        order[starts[k]:starts[k] + size, :] = post_ref[pl.ds(row, size), :]
    members = order.shape[1]
    high, low = halves(order[...].T)
    both[:members, :] = high
    both[members:, :] = low
    for t in range(tiles):
        for copy in copies[t]:
            copy.wait()
        columns = pl.ds(t * tile, tile)
        image_high, image_low = halves(held[:, columns])
        wide = jnp.dot(both[...], image_high, preferred_element_type=jnp.float32)
        rest = jnp.dot(both[:members, :], image_low, preferred_element_type=jnp.float32)
        out_ref[:, columns] = wide[:members] + (wide[members:] + rest)


def weighted(at, post, blocks):
    images, refs = post.shape
    width = blocks[0].shape[1]
    starts = [0]
    for block in blocks[:-1]:
        starts.append(starts[-1] + block.shape[0])
    return pl.pallas_call(
        functools.partial(weighted_kernel, starts),
        out_shape=jax.ShapeDtypeStruct((refs, width), jnp.float32),
        in_specs=[pl.BlockSpec(memory_space=pltpu.SMEM),
                  pl.BlockSpec(memory_space=pltpu.VMEM)]
        + [pl.BlockSpec(memory_space=pl.ANY)] * len(blocks),
        out_specs=pl.BlockSpec(memory_space=pltpu.VMEM),
        scratch_shapes=[pltpu.VMEM((images, width), jnp.float32),
                        pltpu.VMEM((images, refs), jnp.float32),
                        pltpu.VMEM((2 * refs, images), jnp.bfloat16),
                        pltpu.SemaphoreType.DMA((4, len(blocks)))],
        cost_estimate=pl.CostEstimate(
            flops=6 * images * refs * width, bytes_accessed=8 * images * width,
            transcendentals=0),
        name="weighted",
    )(at, post, *blocks)


def step_on_shards(images, references):
    count_z = lax.axis_size("z")
    slices = lax.axis_size("x") * lax.axis_size("core")
    width = images.shape[1] // slices
    here = lax.axis_index("z")
    own = cut(images, lax.axis_index(("x", "core")), width)
    rows = own.shape[0]

    pieces = references.reshape(references.shape[0], slices, width).transpose(1, 0, 2)
    pieces = jnp.broadcast_to(pieces[None], (lax.axis_size("yh"),) + pieces.shape)
    plane_refs = lax.all_to_all(
        pieces.reshape((-1,) + pieces.shape[2:]), OWNERS, 0, 0, tiled=True)
    plane_refs = plane_refs.reshape(-1, width)
    halfnorm = 0.5 * jnp.sum(plane_refs * plane_refs, axis=1)

    partial = jnp.zeros((count_z * rows, plane_refs.shape[0]), jnp.float32)
    blocks, offsets, firsts = [], [], []

    def place(partial, block, offset, first_row):
        scores = lax.dot_general(
            block, plane_refs, (((1,), (1,)), ((), ())),
            precision=HIGHEST, preferred_element_type=jnp.float32) - halfnorm[None, :]
        blocks.append(block)
        offsets.append(offset)
        firsts.append(first_row)
        row = (here + offset) % count_z * rows + first_row
        return lax.dynamic_update_slice_in_dim(partial, scores, row, 0)

    partial = place(partial, own, 0, 0)
    right = left = own
    for step in range(1, count_z // 2 + 1):
        middle = 0
        if step == count_z // 2:
            middle = rows // 2
            right, left = right[:middle], left[middle:]
        right = moved(right, "z", 1)
        left = moved(left, "z", -1)
        partial = place(partial, right, -step, 0)
        partial = place(partial, left, step, middle)

    partial = partial.reshape(count_z, rows, -1)
    scores = jnp.sum(lax.all_to_all(partial, PLANE, 0, 0, tiled=False), axis=0)

    largest = jnp.max(scores, axis=1)
    expon = jnp.exp(scores - largest[:, None])
    totals = jnp.sum(expon, axis=1)
    stats = jnp.stack([largest, totals])
    everyone = lax.all_to_all(
        jnp.broadcast_to(stats[None], (count_z,) + stats.shape), "z", 0, 0, tiled=False)
    top = jnp.max(everyone[:, 0], axis=0)
    total = jnp.sum(everyone[:, 1] * jnp.exp(everyone[:, 0] - top), axis=0)
    post = expon * (jnp.exp(largest - top) / total)[:, None]
    chips = lax.axis_size("yl") * lax.axis_size("x")
    spread = lax.all_to_all(
        jnp.broadcast_to(post[None], (chips,) + post.shape), ("yl", "x"), 0, 0, tiled=False)
    post = lax.all_gather(spread, "core").reshape(-1, post.shape[1])

    at = (here + jnp.array(offsets, jnp.int32)) % count_z * rows + jnp.array(firsts, jnp.int32)
    out = weighted(at, post, blocks)

    owners = lax.axis_size("yh") * slices
    back = lax.all_to_all(out.reshape(owners, -1, width), OWNERS, 0, 0, tiled=False)
    mine_rows = jnp.sum(back.reshape(lax.axis_size("yh"), slices, -1, width), axis=0)
    return mine_rows.transpose(1, 0, 2).reshape(references.shape)


def solution(mesh):
    fine = Mesh(mesh.devices.reshape(16, 2, 2, 4, 2), ("z", "yh", "yl", "x", "core"))
    return jax.shard_map(
        step_on_shards,
        mesh=fine,
        in_specs=(P(("z", "yh"), "yl"), P(("z", "yh", "x", "core"), "yl")),
        out_specs=P(("z", "yh", "x", "core"), "yl"),
        check_vma=False,
    )
```

```python
import functools

import jax
import jax.numpy as jnp
from jax import lax
from jax.experimental import pallas as pl
from jax.experimental.pallas import tpu as pltpu
from jax.sharding import Mesh, PartitionSpec as P


HIGHEST = lax.Precision.HIGHEST
PLANE = ("core", "yl", "x")
OWNERS = ("yh", "x", "core")


def moved(value, axis, steps):
    count = lax.axis_size(axis)
    return lax.ppermute(value, axis, [(i, (i + steps) % count) for i in range(count)])


def cut_kernel(at_ref, images_ref, out_ref, sem):
    width = out_ref.shape[1]
    columns = pl.ds(pl.multiple_of(at_ref[0] * width, width), width)
    copy = pltpu.make_async_copy(images_ref.at[:, columns], out_ref, sem)
    copy.start()
    copy.wait()


def cut(images, which, width):
    return pl.pallas_call(
        cut_kernel,
        out_shape=jax.ShapeDtypeStruct((images.shape[0], width), jnp.float32),
        in_specs=[pl.BlockSpec(memory_space=pltpu.SMEM),
                  pl.BlockSpec(memory_space=pltpu.HBM)],
        out_specs=pl.BlockSpec(memory_space=pltpu.VMEM),
        scratch_shapes=[pltpu.SemaphoreType.DMA(())],
        name="cut",
    )(which.reshape(1).astype(jnp.int32), images)


def halves(value):
    high = value.astype(jnp.bfloat16)
    return high, (value - high.astype(jnp.float32)).astype(jnp.bfloat16)


def split_kernel(starts, at_ref, *refs):
    count = len(starts)
    blocks, (high_ref, low_ref, held, sems) = refs[:count], refs[count:]
    copies = []
    for k, block in enumerate(blocks):
        copies.append(pltpu.make_async_copy(
            block, held.at[pl.ds(starts[k], block.shape[0])], sems.at[k]))
        copies[-1].start()
    for k, block in enumerate(blocks):
        size = block.shape[0]
        rows = pl.ds(pl.multiple_of(at_ref[k], 16), size)
        copies[k].wait()
        high_ref[rows, :], low_ref[rows, :] = halves(held[starts[k]:starts[k] + size, :])


def split(at, blocks):
    width = blocks[0].shape[1]
    starts = [0]
    for block in blocks:
        starts.append(starts[-1] + block.shape[0])
    images = starts.pop()
    half = jax.ShapeDtypeStruct((images, width), jnp.bfloat16)
    return pl.pallas_call(
        functools.partial(split_kernel, starts),
        out_shape=(half, half),
        in_specs=[pl.BlockSpec(memory_space=pltpu.SMEM)]
        + [pl.BlockSpec(memory_space=pl.ANY)] * len(blocks),
        out_specs=(pl.BlockSpec(memory_space=pltpu.VMEM),) * 2,
        scratch_shapes=[pltpu.VMEM((images, width), jnp.float32),
                        pltpu.SemaphoreType.DMA((len(blocks),))],
        cost_estimate=pl.CostEstimate(
            flops=4 * images * width, bytes_accessed=8 * images * width, transcendentals=0),
        name="split",
    )(at, *blocks)


def weighted_kernel(post_ref, high_ref, low_ref, out_ref, both):
    members = post_ref.shape[1]

    @pl.when(pl.program_id(0) == 0)
    def _():
        high, low = halves(post_ref[...].T)
        both[:members, :] = high
        both[members:, :] = low

    wide = jnp.dot(both[...], high_ref[...], preferred_element_type=jnp.float32)
    rest = jnp.dot(both[:members, :], low_ref[...], preferred_element_type=jnp.float32)
    out_ref[...] = wide[:members] + (wide[members:] + rest)


def weighted(post, high, low):
    images, refs = post.shape
    width = high.shape[1]
    tile = 256
    return pl.pallas_call(
        weighted_kernel,
        out_shape=jax.ShapeDtypeStruct((refs, width), jnp.float32),
        grid=(width // tile,),
        in_specs=[pl.BlockSpec((images, refs), lambda t: (0, 0)),
                  pl.BlockSpec((images, tile), lambda t: (0, t)),
                  pl.BlockSpec((images, tile), lambda t: (0, t))],
        out_specs=pl.BlockSpec((refs, tile), lambda t: (0, t)),
        scratch_shapes=[pltpu.VMEM((2 * refs, images), jnp.bfloat16)],
        cost_estimate=pl.CostEstimate(
            flops=6 * images * refs * width, bytes_accessed=4 * images * width,
            transcendentals=0),
        name="weighted",
    )(post, high, low)


def step_on_shards(images, references):
    count_z = lax.axis_size("z")
    slices = lax.axis_size("x") * lax.axis_size("core")
    width = images.shape[1] // slices
    here = lax.axis_index("z")
    own = cut(images, lax.axis_index(("x", "core")), width)
    rows = own.shape[0]

    pieces = references.reshape(references.shape[0], slices, width).transpose(1, 0, 2)
    pieces = jnp.broadcast_to(pieces[None], (lax.axis_size("yh"),) + pieces.shape)
    plane_refs = lax.all_to_all(
        pieces.reshape((-1,) + pieces.shape[2:]), OWNERS, 0, 0, tiled=True)
    plane_refs = plane_refs.reshape(-1, width)
    halfnorm = 0.5 * jnp.sum(plane_refs * plane_refs, axis=1)

    partial = jnp.zeros((count_z * rows, plane_refs.shape[0]), jnp.float32)
    blocks, offsets, firsts = [], [], []

    def place(partial, block, offset, first_row):
        scores = lax.dot_general(
            block, plane_refs, (((1,), (1,)), ((), ())),
            precision=HIGHEST, preferred_element_type=jnp.float32) - halfnorm[None, :]
        blocks.append(block)
        offsets.append(offset)
        firsts.append(first_row)
        row = (here + offset) % count_z * rows + first_row
        return lax.dynamic_update_slice_in_dim(partial, scores, row, 0)

    partial = place(partial, own, 0, 0)
    right = left = own
    for step in range(1, count_z // 2 + 1):
        middle = 0
        if step == count_z // 2:
            middle = rows // 2
            right, left = right[:middle], left[middle:]
        right = moved(right, "z", 1)
        left = moved(left, "z", -1)
        partial = place(partial, right, -step, 0)
        partial = place(partial, left, step, middle)

    partial = partial.reshape(count_z, rows, -1)
    at = (here + jnp.array(offsets, jnp.int32)) % count_z * rows + jnp.array(firsts, jnp.int32)
    high, low = split(at, blocks)
    everything = lax.all_to_all(partial, PLANE, 0, 0, tiled=False)
    scores = jnp.sum(everything, axis=0)

    largest = jnp.max(scores, axis=1)
    expon = jnp.exp(scores - largest[:, None])
    totals = jnp.sum(expon, axis=1)
    stats = jnp.stack([largest, totals])
    everyone = lax.all_to_all(
        jnp.broadcast_to(stats[None], (count_z,) + stats.shape), "z", 0, 0, tiled=False)
    top = jnp.max(everyone[:, 0], axis=0)
    total = jnp.sum(everyone[:, 1] * jnp.exp(everyone[:, 0] - top), axis=0)
    post = expon * (jnp.exp(largest - top) / total)[:, None]
    chips = lax.axis_size("yl") * lax.axis_size("x")
    spread = lax.all_to_all(
        jnp.broadcast_to(post[None], (chips,) + post.shape), ("yl", "x"), 0, 0, tiled=False)
    post = lax.all_gather(spread, "core").reshape(-1, post.shape[1])

    out = weighted(post, high, low)

    owners = lax.axis_size("yh") * slices
    back = lax.all_to_all(out.reshape(owners, -1, width), OWNERS, 0, 0, tiled=False)
    mine_rows = jnp.sum(back.reshape(lax.axis_size("yh"), slices, -1, width), axis=0)
    return mine_rows.transpose(1, 0, 2).reshape(references.shape)


def solution(mesh):
    fine = Mesh(mesh.devices.reshape(16, 2, 2, 4, 2), ("z", "yh", "yl", "x", "core"))
    return jax.shard_map(
        step_on_shards,
        mesh=fine,
        in_specs=(P(("z", "yh"), "yl"), P(("z", "yh", "x", "core"), "yl")),
        out_specs=P(("z", "yh", "x", "core"), "yl"),
        check_vma=False,
    )
```

```python
import functools

import jax
import jax.numpy as jnp
from jax import lax
from jax.experimental import pallas as pl
from jax.experimental.pallas import tpu as pltpu
from jax.sharding import Mesh, PartitionSpec as P


HIGHEST = lax.Precision.HIGHEST
PLANE = ("core", "yl", "x")
OWNERS = ("yh", "x", "core")


def moved(value, axis, steps):
    count = lax.axis_size(axis)
    return lax.ppermute(value, axis, [(i, (i + steps) % count) for i in range(count)])


def cut_kernel(at_ref, images_ref, out_ref, sem):
    width = out_ref.shape[1]
    columns = pl.ds(pl.multiple_of(at_ref[0] * width, width), width)
    copy = pltpu.make_async_copy(images_ref.at[:, columns], out_ref, sem)
    copy.start()
    copy.wait()


def cut(images, which, width):
    return pl.pallas_call(
        cut_kernel,
        out_shape=jax.ShapeDtypeStruct((images.shape[0], width), jnp.float32),
        in_specs=[pl.BlockSpec(memory_space=pltpu.SMEM),
                  pl.BlockSpec(memory_space=pltpu.HBM)],
        out_specs=pl.BlockSpec(memory_space=pltpu.VMEM),
        scratch_shapes=[pltpu.SemaphoreType.DMA(())],
        name="cut",
    )(which.reshape(1).astype(jnp.int32), images)


def halves(value):
    high = value.astype(jnp.bfloat16)
    return high, (value - high.astype(jnp.float32)).astype(jnp.bfloat16)


def split_kernel(starts, at_ref, *refs):
    count = len(starts)
    blocks, (high_ref, low_ref, held, sems) = refs[:count], refs[count:]
    copies = []
    for k, block in enumerate(blocks):
        copies.append(pltpu.make_async_copy(
            block, held.at[pl.ds(starts[k], block.shape[0])], sems.at[k]))
        copies[-1].start()
    for k, block in enumerate(blocks):
        size = block.shape[0]
        rows = pl.ds(pl.multiple_of(at_ref[k], 16), size)
        copies[k].wait()
        high_ref[rows, :], low_ref[rows, :] = halves(held[starts[k]:starts[k] + size, :])


def split(at, blocks):
    width = blocks[0].shape[1]
    starts = [0]
    for block in blocks:
        starts.append(starts[-1] + block.shape[0])
    images = starts.pop()
    half = jax.ShapeDtypeStruct((images, width), jnp.bfloat16)
    return pl.pallas_call(
        functools.partial(split_kernel, starts),
        out_shape=(half, half),
        in_specs=[pl.BlockSpec(memory_space=pltpu.SMEM)]
        + [pl.BlockSpec(memory_space=pl.ANY)] * len(blocks),
        out_specs=(pl.BlockSpec(memory_space=pltpu.VMEM),) * 2,
        scratch_shapes=[pltpu.VMEM((images, width), jnp.float32),
                        pltpu.SemaphoreType.DMA((len(blocks),))],
        cost_estimate=pl.CostEstimate(
            flops=4 * images * width, bytes_accessed=8 * images * width, transcendentals=0),
        name="split",
    )(at, *blocks)


def weighted_kernel(post_ref, high_ref, low_ref, out_ref, both):
    members = post_ref.shape[1]

    @pl.when(pl.program_id(0) == 0)
    def _():
        high, low = halves(post_ref[...].T)
        both[:members, :] = high
        both[members:, :] = low

    wide = jnp.dot(both[...], high_ref[...], preferred_element_type=jnp.float32)
    rest = jnp.dot(both[:members, :], low_ref[...], preferred_element_type=jnp.float32)
    out_ref[...] = wide[:members] + (wide[members:] + rest)


def weighted(post, high, low):
    images, refs = post.shape
    width = high.shape[1]
    tile = 256
    return pl.pallas_call(
        weighted_kernel,
        out_shape=jax.ShapeDtypeStruct((refs, width), jnp.float32),
        grid=(width // tile,),
        in_specs=[pl.BlockSpec((images, refs), lambda t: (0, 0)),
                  pl.BlockSpec((images, tile), lambda t: (0, t)),
                  pl.BlockSpec((images, tile), lambda t: (0, t))],
        out_specs=pl.BlockSpec((refs, tile), lambda t: (0, t)),
        scratch_shapes=[pltpu.VMEM((2 * refs, images), jnp.bfloat16)],
        cost_estimate=pl.CostEstimate(
            flops=6 * images * refs * width, bytes_accessed=4 * images * width,
            transcendentals=0),
        name="weighted",
    )(post, high, low)


def step_on_shards(images, references):
    count_z = lax.axis_size("z")
    slices = lax.axis_size("x") * lax.axis_size("core")
    width = images.shape[1] // slices
    here = lax.axis_index("z")
    own = cut(images, lax.axis_index(("x", "core")), width)
    rows = own.shape[0]

    pieces = references.reshape(references.shape[0], slices, width).transpose(1, 0, 2)
    pieces = jnp.broadcast_to(pieces[None], (lax.axis_size("yh"),) + pieces.shape)
    plane_refs = lax.all_to_all(
        pieces.reshape((-1,) + pieces.shape[2:]), OWNERS, 0, 0, tiled=True)
    plane_refs = plane_refs.reshape(-1, width)

    blocks, offsets, firsts = [], [], []

    def keep(block, offset, first_row):
        blocks.append(block)
        offsets.append(offset)
        firsts.append(first_row)

    keep(own, 0, 0)
    right = left = own
    for step in range(1, count_z // 2 + 1):
        middle = 0
        if step == count_z // 2:
            middle = rows * 2 // 3
            right, left = right[:middle], left[middle:]
        right = moved(right, "z", 1)
        left = moved(left, "z", -1)
        keep(right, -step, 0)
        keep(left, step, middle)

    read = list(blocks)
    plane_refs, read[3] = lax.optimization_barrier((plane_refs, blocks[3]))
    halfnorm = 0.5 * jnp.sum(plane_refs * plane_refs, axis=1)
    partial = jnp.zeros((count_z * rows, plane_refs.shape[0]), jnp.float32)
    for block, offset, first_row in zip(read, offsets, firsts):
        scores = lax.dot_general(
            block, plane_refs, (((1,), (1,)), ((), ())),
            precision=HIGHEST, preferred_element_type=jnp.float32) - halfnorm[None, :]
        row = (here + offset) % count_z * rows + first_row
        partial = lax.dynamic_update_slice_in_dim(partial, scores, row, 0)

    partial = partial.reshape(count_z, rows, -1)
    at = (here + jnp.array(offsets, jnp.int32)) % count_z * rows + jnp.array(firsts, jnp.int32)
    high, low = split(at, blocks)
    scores = jnp.sum(lax.all_to_all(partial, PLANE, 0, 0, tiled=False), axis=0)

    largest = jnp.max(scores, axis=1)
    expon = jnp.exp(scores - largest[:, None])
    totals = jnp.sum(expon, axis=1)
    stats = jnp.stack([largest, totals])
    everyone = lax.all_to_all(
        jnp.broadcast_to(stats[None], (count_z,) + stats.shape), "z", 0, 0, tiled=False)
    top = jnp.max(everyone[:, 0], axis=0)
    total = jnp.sum(everyone[:, 1] * jnp.exp(everyone[:, 0] - top), axis=0)
    post = expon * (jnp.exp(largest - top) / total)[:, None]
    chips = lax.axis_size("yl") * lax.axis_size("x")
    spread = lax.all_to_all(
        jnp.broadcast_to(post[None], (chips,) + post.shape), ("yl", "x"), 0, 0, tiled=False)
    post = lax.all_gather(spread, "core").reshape(-1, post.shape[1])

    out = weighted(post, high, low)

    owners = lax.axis_size("yh") * slices
    back = lax.all_to_all(out.reshape(owners, -1, width), OWNERS, 0, 0, tiled=False)
    mine_rows = jnp.sum(back.reshape(lax.axis_size("yh"), slices, -1, width), axis=0)
    return mine_rows.transpose(1, 0, 2).reshape(references.shape)


def solution(mesh):
    fine = Mesh(mesh.devices.reshape(16, 2, 2, 4, 2), ("z", "yh", "yl", "x", "core"))
    return jax.shard_map(
        step_on_shards,
        mesh=fine,
        in_specs=(P(("z", "yh"), "yl"), P(("z", "yh", "x", "core"), "yl")),
        out_specs=P(("z", "yh", "x", "core"), "yl"),
        check_vma=False,
    )
```
